32 devices in a mesh: ind: 4 (over x, core), mark: 4 (over z), chip: 2 (over y).
Axes of the slice: x: 2, y: 2, z: 4, core: 2. Of those that a mesh axis runs over, the one named last changes fastest.
Arguments:
- genotypes: bfloat16 [8192, 8192], P(('ind', 'chip'), 'mark'), may hold values from -0.1875 to 0.1875
- residual: float32 [8192, 1024], P(('ind', 'chip'), 'mark'), as said below
- posterior_inverse: bfloat16 [8, 1024, 1024], P('mark'), as said below
- gibbs_noise: bfloat16 [4, 8192, 256], P(None, 'mark'), may hold values from -6 to 6
- visit_order: int32 [4, 4, 2], P(None, 'mark'), may hold values from 0 to 1, each once within a row
Outputs:
- residual_after: float32 [8192, 1024], P(('ind', 'chip'), 'mark')
- effect_changes: float32 [4, 8192, 256], P(None, 'mark')
The draws below stay inside these ranges and needn't reach their ends.
Inputs may be any that keep to these rules, and one draw needn't show every extreme that they name: `visit_order`: each row names each of the 2 marker blocks of one cycle position once. `residual`: finite real values. `posterior_inverse`: the diagonal entries are positive.
All inputs are finite; a program needn't handle non-finite values.
Results may differ from the reference program's by a relative error of at most 0.005.
Values sent between devices are 32-bit elements; how exact they have to be, the bound alone decides.
A program may use at most 128 MiB of HBM per device.

```python
import math
import jax
import jax.numpy as jnp
from jax import lax

MB = 1024
TB = 256
BLK_DEV = 2
TRAITS = 1024
STOPS = 4
MBLOCKS = 8
MARKERS = 8192
INDIV = 8192
N_MARK = 4


def draw_residual(key, part):
    first, second, third = jax.random.split(jax.random.fold_in(key, 11), 3)
    rows = jnp.arange(INDIV, dtype=jnp.float32) / INDIV
    row_scale = jnp.exp(jnp.log(3.0) * rows + jax.random.uniform(first, (INDIV,), jnp.float32, -1.15, 1.15))
    col_scale = jnp.exp(jax.random.uniform(second, (TRAITS,), jnp.float32, -1.15, 1.15))
    base = jnp.clip(jax.random.normal(third, (INDIV, TRAITS), jnp.float32), -6.0, 6.0)
    return (0.3 * base * row_scale[:, None] * col_scale[None, :]).astype(jnp.float32)


def draw_posterior_inverse(key, part):
    first, second = jax.random.split(jax.random.fold_in(key, 23), 2)
    diagonal = jax.random.uniform(first, (MBLOCKS, MB), jnp.float32, 0.4, 0.8)
    offdiag = jax.random.normal(second, (MBLOCKS, MB, MB), jnp.float32) * (0.15 / math.sqrt(MB))
    matrix = offdiag * (1.0 - jnp.eye(MB, dtype=jnp.float32))[None] + jnp.eye(MB, dtype=jnp.float32)[None] * diagonal[:, :, None]
    return (matrix * MB).astype(jnp.bfloat16)


def steps_of(key, dims, cuts, low, largest):
    def one(axis_at, parts):
        steps = jax.random.uniform(jax.random.fold_in(jax.random.fold_in(key, 6), axis_at), (parts,), jnp.float32, low / len(cuts), largest / len(cuts))
        return jnp.repeat(jnp.exp(steps), dims[axis_at] // parts).reshape((-1,) + (1,) * (len(dims) - axis_at - 1))

    gain = one(*cuts[0])
    for cut in cuts[1:]:
        gain = gain * one(*cut)
    return gain


def gaussian(own_key, shape, scale, limit, cuts=(), held_as=jnp.bfloat16):
    gain = steps_of(own_key, shape, cuts, -0.22, 0.18) if cuts else 1.0
    values = jax.random.normal(own_key, shape, jnp.float32) * scale * gain
    return jnp.minimum(jnp.maximum(values, -limit), limit).astype(held_as)


def setup_inputs(seed: int = 0) -> dict:
    keys = jax.random.split(jax.random.key(seed), 6)
    return {
        "genotypes": gaussian(keys[0], (INDIV, MARKERS), MB ** -0.5, 0.1875, ((0, 8), (1, 4))),
        "residual": draw_residual(jax.random.fold_in(keys[5], 71), 0),
        "posterior_inverse": draw_posterior_inverse(jax.random.fold_in(keys[5], 71), 0),
        "gibbs_noise": gaussian(keys[3], (STOPS, MARKERS, TB), 1.0, 6.0, ((1, 4),)),
        "visit_order": jax.vmap(lambda own: jax.random.permutation(own, BLK_DEV))(jax.random.split(keys[4], STOPS * N_MARK)).reshape((STOPS, N_MARK, BLK_DEV)).astype(jnp.int32),
    }


epsilon = 1e-05

def reference(genotypes, residual, posterior_inverse, gibbs_noise, visit_order):
    current_all = residual
    change_list = []
    for stop_idx in range(STOPS):
        stop_changes = jnp.zeros((MARKERS, TB), jnp.float32)
        for cycle_pos in range(N_MARK):
            trait_blk = (cycle_pos - stop_idx) % N_MARK
            current = current_all[:, trait_blk * TB:(trait_blk + 1) * TB]
            for visit_pos in range(BLK_DEV):
                local_blk = visit_order[stop_idx, cycle_pos, visit_pos].astype(jnp.int32)
                global_blk = (local_blk + cycle_pos * BLK_DEV).astype(jnp.int32)
                columns = lax.dynamic_slice_in_dim(genotypes, (global_blk * MB).astype(jnp.int32), MB, 1)
                scores = lax.dot_general(columns, current.astype(jnp.bfloat16), (((0,), (0,)), ((), ())), preferred_element_type=jnp.float32)
                spread = lax.optimization_barrier(jnp.sum(current * current, axis=0)) / INDIV
                inverse = lax.dynamic_index_in_dim(posterior_inverse, global_blk, 0, keepdims=False)
                scaled = (scores / INDIV).astype(jnp.bfloat16)
                mean_part = jnp.dot(inverse, scaled, preferred_element_type=jnp.float32)
                diag_part = jnp.diagonal(inverse).astype(jnp.float32)
                start_row = (cycle_pos * BLK_DEV + visit_pos) * MB
                noise_rows = gibbs_noise[stop_idx, start_row:start_row + MB, :].astype(jnp.float32)
                change = mean_part + jnp.sqrt(diag_part[:, None] * (spread[None, :] + epsilon) / INDIV) * noise_rows
                stop_changes = lax.dynamic_update_slice_in_dim(stop_changes, change, (global_blk * MB).astype(jnp.int32), 0)
                current = current - jnp.dot(columns, change.astype(jnp.bfloat16), preferred_element_type=jnp.float32)
            current_all = current_all.at[:, trait_blk * TB:(trait_blk + 1) * TB].set(current)
        change_list.append(stop_changes)
    return (current_all, jnp.stack(change_list))
```

```python
import functools

import jax
import jax.numpy as jnp
from jax import lax
from jax.experimental import pallas as pl
from jax.experimental.pallas import tpu as pltpu
from jax.sharding import PartitionSpec as P

epsilon = 1e-05
MESH = pl.DeviceIdType.MESH
CHUNKS = 4
PERIOD = 6
ORDER = (
    ("m", 3),
    ("c", 4),
    ("l", 5),
    ("d", 2),
    ("b", 3),
    ("a", 0),
    ("N", 0),
    ("c", 1),
    ("G", 1),
    ("d", 4),
    ("b", 0),
    ("V", 0),
)
LANES = 128
SUB = 8


def bits_of(n):
    steps = []
    s = 1
    while s < n:
        steps.append(s)
        s *= 2
    return steps


def kernel(
    cfg,
    order_ref,
    geno_hbm,
    resid_hbm,
    inv_hbm,
    noise_hbm,
    after_hbm,
    change_hbm,
    geno_ref,
    geno_t,
    resid_ref,
    inv_ref,
    inv_t,
    noise_raw,
    noise_ref,
    droot_ref,
    change_ref,
    ebuf,
    part,
    r1,
    rx,
    acc,
    full,
    meanp,
    stash,
    in_sem,
    out_sem,
    after_sem,
    p1s,
    p1r,
    xs,
    xr,
    fs,
    fr,
    zs,
    zr,
):
    n_ind, n_mark, n_chip, chunks, stops, count, block, levels = cfg
    tc = ebuf.shape[2]
    half = block // 2
    nb = half // LANES // levels
    seg_rows = nb * tc
    body_rows = levels * seg_rows
    groups = tc // SUB
    ind = lax.axis_index("ind")
    mark = lax.axis_index("mark")
    y = lax.axis_index("chip")
    core = lax.rem(ind, 2)
    x = lax.div(ind, 2)
    role = lax.rem(core + x + y, 2)
    other = 1 - role
    partner = {"ind": ind + 1 - 2 * core}
    nxt = {"mark": lax.rem(mark + 1, n_mark)}
    prv = {"mark": lax.rem(mark + n_mark - 1, n_mark)}

    def peer(axis, s):
        nx, ny = x, y
        if axis == "x":
            nx = x + s * (1 - 2 * lax.rem(lax.div(x, s), 2))
        else:
            ny = y + s * (1 - 2 * lax.rem(lax.div(y, s), 2))
        return {"ind": nx * 2 + lax.rem(role + nx + ny, 2), "chip": ny}

    peers = [peer("x", s) for s in bits_of(n_ind // 2)] + [peer("y", s) for s in bits_of(n_chip)]

    blocks = geno_ref.shape[0]
    per_visit = chunks // blocks
    piece = noise_ref.shape[3]
    loads = [pltpu.make_async_copy(resid_hbm, resid_ref, in_sem.at[0])]
    for k in range(blocks):
        loads.append(
            pltpu.make_async_copy(
                geno_hbm.at[:, k * block : (k + 1) * block], geno_ref.at[k], in_sem.at[1 + k]
            )
        )
    loads.append(pltpu.make_async_copy(noise_hbm, noise_raw, in_sem.at[1 + blocks]))
    loads.append(pltpu.make_async_copy(inv_hbm, inv_ref, in_sem.at[2 + blocks]))
    for load in loads:
        load.start()

    barrier = pltpu.get_barrier_semaphore()
    for dev in [partner, nxt, prv] + peers:
        pl.semaphore_signal(barrier, inc=1, device_id=dev, device_id_type=MESH)

    loads[0].wait()
    flipped = resid_ref[...].T
    for c in range(chunks):
        ebuf[0, c] = flipped[c * tc : (c + 1) * tc]
    for k in range(blocks):
        loads[1 + k].wait()
    pl.semaphore_wait(barrier, 3 + levels)

    def copy(src, dst, ssem, rsem, dev):
        return pltpu.make_async_remote_copy(
            src_ref=src, dst_ref=dst, send_sem=ssem, recv_sem=rsem, device_id=dev, device_id_type=MESH
        )

    def hop(stop, c):
        return copy(ebuf.at[stop, c], ebuf.at[stop + 1, c], zs.at[stop, c], zr.at[stop, c], nxt)

    def pair(c):
        return copy(part.at[c, other], r1.at[c], p1s.at[c], p1r.at[c], partner)

    def rows_of(g):
        return pl.ds(g * seg_rows, seg_rows + (SUB if g == levels - 1 else 0))

    def source(c, p):
        return part.at[c, role] if p == 0 else acc.at[c, p - 1]

    def swap(c, p, g):
        rows = rows_of(g)
        return copy(
            source(c, p).at[rows], rx.at[c, p, rows], xs.at[c, p, g], xr.at[c, p, g], peers[(g + p) % levels]
        )

    def forward(c):
        return copy(
            full.at[c, role, pl.ds(0, body_rows)],
            full.at[c, role, pl.ds(0, body_rows)],
            fs.at[c],
            fr.at[c],
            partner,
        )

    lane = lax.broadcasted_iota(jnp.int32, (SUB, LANES), 1)

    def bit(s):
        return lax.rem(lax.div(lane, s), 2) == 1

    def fold(tot):
        parts = [tot[SUB * g : SUB * (g + 1)] for g in range(groups)]
        s = LANES // 2
        while len(parts) > 1:
            take = bit(s)
            parts = [
                jnp.where(take, a + pltpu.roll(a, s, 1), b + pltpu.roll(b, LANES - s, 1))
                for a, b in zip(parts[::2], parts[1::2])
            ]
            s //= 2
        return parts[0]

    def unfold(tile):
        sums = []
        for g in range(groups):
            s, r, value = LANES // 2, g, tile
            for _ in bits_of(groups):
                value = jnp.where(bit(s) if r % 2 == 0 else jnp.logical_not(bit(s)), value, 0.0)
                s, r = s // 2, r // 2
            sums.append(jnp.sum(value, axis=1, keepdims=True))
        return jnp.concatenate(sums, axis=0)

    def put(c, h, s):
        for i in range(levels * nb):
            part[c, h, i * tc : (i + 1) * tc, :] = s[:, i * LANES : (i + 1) * LANES]

    def scaled_half(c, h):
        return jnp.concatenate(
            [(full[c, h, i * tc : (i + 1) * tc, :] * (1.0 / count)).astype(jnp.bfloat16) for i in range(levels * nb)],
            axis=1,
        )

    def span(h):
        return pl.ds(pl.multiple_of(h * half, half), half)

    def score(stop, j, c):
        k = order_ref[stop, 0, j]
        e = ebuf[stop, c]
        eb = e.astype(jnp.bfloat16)
        put(c, other, jnp.dot(eb, geno_ref[k, :, span(other)], preferred_element_type=jnp.float32))
        sq = e * e
        tot = sq[:, :LANES]
        for i in range(1, sq.shape[1] // LANES):
            tot = tot + sq[:, i * LANES : (i + 1) * LANES]
        tile = fold(tot)
        part[c, 0, body_rows:, :] = tile
        part[c, 1, body_rows:, :] = tile
        pair(c).start()
        put(c, role, jnp.dot(eb, geno_ref[k, :, span(role)], preferred_element_type=jnp.float32))

    def phase_a(stop, c):
        @pl.when(stop > 0)
        def _():
            hop(stop - 1, c).wait_recv()

        score(stop, 0, c)

    def phase_b(stop, c):
        pair(c).wait_recv()
        part[c, role] = part[c, role] + r1[c]
        for g in range(levels):
            swap(c, 0, g).start()

    def phase_c(stop, c):
        for p in range(levels - 1):
            for g in range(levels):
                swap(c, p, g).wait_recv()
            acc[c, p] = source(c, p)[...] + rx[c, p]
            for g in range(levels):
                swap(c, p + 1, g).start()
        pair(c).wait_send()

    def phase_d(stop, j, c):
        p = levels - 1
        for g in range(levels):
            swap(c, p, g).wait_recv()
        full[c, role] = source(c, p)[...] + rx[c, p]
        forward(c).start()
        k = order_ref[stop, 0, j]
        meanp[c] = jnp.dot(scaled_half(c, role), inv_t[k, span(role), :], preferred_element_type=jnp.float32)
        for p in range(levels):
            for g in range(levels):
                swap(c, p, g).wait_send()

    def phase_e(stop, j, c):
        k = order_ref[stop, 0, j]
        spread = unfold(full[c, role, body_rows:, :]) * (1.0 / count)
        root = jnp.sqrt((spread + epsilon) * (1.0 / count))
        noise = jnp.concatenate(
            [
                noise_ref[stop, j * per_visit + i, pl.ds(pl.multiple_of(c * tc, tc), tc), :]
                for i in range(per_visit)
            ],
            axis=1,
        ).astype(jnp.float32)
        forward(c).wait_recv()
        mean = meanp[c] + jnp.dot(
            scaled_half(c, other), inv_t[k, span(other), :], preferred_element_type=jnp.float32
        )
        change = mean + (root * droot_ref[k]) * noise
        stash[c, j] = change
        ebuf[stop, c] = ebuf[stop, c] - jnp.dot(
            change.astype(jnp.bfloat16), geno_t[k], preferred_element_type=jnp.float32
        )

    def at(x, fn):
        stop, c = lax.div(x, PERIOD), lax.rem(x, PERIOD)

        @pl.when((x >= 0) & (c < chunks) & (stop < stops))
        def _():
            fn(stop, c)

    def out_copy(stop, c):
        return pltpu.make_async_copy(change_ref.at[stop, :, c], change_hbm.at[stop, :, c], out_sem.at[stop, c])

    def last(stop, c):
        phase_e(stop, 1, c)
        hop(stop, c).start()
        forward(c).wait_send()
        first = order_ref[stop, 0, 0]
        change_ref[stop, 0, c] = stash[c, first]
        change_ref[stop, 1, c] = stash[c, 1 - first]
        out_copy(stop, c).start()

    def middle(stop, c):
        phase_e(stop, 0, c)
        score(stop, 1, c)
        forward(c).wait_send()

    def flip(stop, i):
        noise_ref[stop, i] = noise_raw[stop, pl.ds(pl.multiple_of(i * piece, piece), piece), :].T

    def turn(src, dst):
        for k in range(blocks):

            def one(i, z):
                cols = pl.ds(pl.multiple_of(i * LANES, LANES), LANES)
                dst[k, cols, :] = src[k, :, cols].T
                return z

            lax.fori_loop(0, block // LANES, one, 0)

    def prepare_noise():
        loads[1 + blocks].wait()
        lax.fori_loop(0, chunks, lambda i, x: (flip(0, i), x)[1], 0)

    def prepare_inverse():
        loads[2 + blocks].wait()
        turn(inv_ref, inv_t)
        eye = lax.broadcasted_iota(jnp.int32, (LANES, LANES), 0) == lax.broadcasted_iota(
            jnp.int32, (LANES, LANES), 1
        )
        for k in range(blocks):
            for i in range(0, block, LANES):
                tile = inv_ref[k, i : i + LANES, i : i + LANES].astype(jnp.float32)
                diag = jnp.sum(jnp.where(eye, tile, 0.0), axis=0, keepdims=True)
                droot_ref[k, :, i : i + LANES] = jnp.sqrt(diag)

    def prepare_genotypes():
        turn(geno_ref, geno_t)

    once = {"N": prepare_noise, "V": prepare_inverse, "G": prepare_genotypes}
    phases = {
        "a": phase_a,
        "b": phase_b,
        "c": phase_c,
        "m": middle,
        "l": last,
    }

    def body(t, carry):
        seen = 0
        for name, delay in ORDER:
            if name in once:
                pl.when(t == delay)(once[name])
            elif name == "d":
                visit = 0 if delay == min(d for n, d in ORDER if n == "d") else 1
                at(t - delay, lambda stop, c, visit=visit: phase_d(stop, visit, c))
            else:
                at(t - delay, phases[name])
        at(t + PERIOD, flip)
        return carry

    lax.fori_loop(0, PERIOD * (stops - 1) + chunks + max(delay for _, delay in ORDER), body, 0)

    def finish(c):
        return pltpu.make_async_copy(ebuf.at[stops, c], after_hbm.at[c], after_sem.at[c])

    for c in range(chunks):
        hop(stops - 1, c).wait_recv()
        finish(c).start()
    for c in range(chunks):
        for stop in range(stops):
            out_copy(stop, c).wait()
            hop(stop, c).wait_send()
        finish(c).wait()


def local(mesh_shape, genotypes, residual, posterior_inverse, gibbs_noise, visit_order):
    n_ind, n_mark, n_chip = mesh_shape
    levels = len(bits_of(n_ind // 2)) + len(bits_of(n_chip))
    people, traits = residual.shape
    count = people * n_ind * n_chip
    blocks, block = posterior_inverse.shape[:2]
    stops = gibbs_noise.shape[0]
    chunks = CHUNKS
    tc = traits // chunks
    rows = block // 2 // LANES * tc + SUB
    f32, bf16 = jnp.float32, jnp.bfloat16
    cfg = (n_ind, n_mark, n_chip, chunks, stops, count, block, levels)
    hbm = pl.BlockSpec(memory_space=pl.ANY)
    dma = pltpu.SemaphoreType.DMA
    after, changes = pl.pallas_call(
        functools.partial(kernel, cfg),
        out_shape=(
            jax.ShapeDtypeStruct((chunks, tc, people), f32),
            jax.ShapeDtypeStruct((stops, blocks, chunks, tc, block), f32),
        ),
        in_specs=[pl.BlockSpec(memory_space=pltpu.SMEM)] + [hbm] * 4,
        out_specs=(hbm, hbm),
        scratch_shapes=[
            pltpu.VMEM((blocks, people, block), bf16),
            pltpu.VMEM((blocks, block, people), bf16),
            pltpu.VMEM((people, traits), f32),
            pltpu.VMEM((blocks, block, block), bf16),
            pltpu.VMEM((blocks, block, block), bf16),
            pltpu.VMEM((stops, blocks * block, traits), bf16),
            pltpu.VMEM((stops, chunks, traits, blocks * block // chunks), bf16),
            pltpu.VMEM((blocks, 1, block), f32),
            pltpu.VMEM((stops, blocks, chunks, tc, block), f32),
            pltpu.VMEM((stops + 1, chunks, tc, people), f32),
            pltpu.VMEM((chunks, 2, rows, LANES), f32),
            pltpu.VMEM((chunks, rows, LANES), f32),
            pltpu.VMEM((chunks, levels, rows, LANES), f32),
            pltpu.VMEM((chunks, levels - 1, rows, LANES), f32),
            pltpu.VMEM((chunks, 2, rows, LANES), f32),
            pltpu.VMEM((chunks, tc, block), f32),
            pltpu.VMEM((chunks, blocks, tc, block), f32),
            dma((3 + blocks,)),
            dma((stops, chunks)),
            dma((chunks,)),
            dma((chunks,)),
            dma((chunks,)),
            dma((chunks, levels, levels)),
            dma((chunks, levels, levels)),
            dma((chunks,)),
            dma((chunks,)),
            dma((stops, chunks)),
            dma((stops, chunks)),
        ],
        compiler_params=pltpu.CompilerParams(
            collective_id=0, has_side_effects=True, vmem_limit_bytes=60 * 1024 * 1024
        ),
    )(visit_order, genotypes, residual, posterior_inverse, gibbs_noise)
    after = after.reshape(traits, people).T
    changes = changes.reshape(stops, blocks, traits, block).transpose(0, 1, 3, 2)
    return after, changes.reshape(stops, blocks * block, traits)


def solution(mesh):
    in_specs = (
        P(("ind", "chip"), "mark"),
        P(("ind", "chip"), "mark"),
        P("mark", None, None),
        P(None, "mark", None),
        P(None, "mark", None),
    )
    out_specs = (P(("ind", "chip"), "mark"), P(None, "mark", None))
    shape = (mesh.shape["ind"], mesh.shape["mark"], mesh.shape["chip"])
    return jax.shard_map(
        functools.partial(local, shape), mesh=mesh, in_specs=in_specs, out_specs=out_specs, check_vma=False
    )
```

```python
import functools

import jax
import jax.numpy as jnp
from jax import lax
from jax.experimental import pallas as pl
from jax.experimental.pallas import tpu as pltpu
from jax.sharding import PartitionSpec as P

epsilon = 1e-05
MESH = pl.DeviceIdType.MESH
CHUNKS = 4
PERIOD = 5
ORDER = (
    ("G", 1),
    ("m", 2),
    ("c", 1),
    ("a", 0),
    ("N", 0),
    ("b", 2),
    ("b", 0),
    ("e", 3),
    ("V", 1),
    ("d", 1),
    ("l", 3),
    ("c", 2),
)
LANES = 128
SUB = 8


def bits_of(n):
    steps = []
    s = 1
    while s < n:
        steps.append(s)
        s *= 2
    return steps


def kernel(
    cfg,
    order_ref,
    geno_hbm,
    resid_hbm,
    inv_hbm,
    noise_hbm,
    after_hbm,
    change_hbm,
    geno_ref,
    geno_t,
    resid_ref,
    inv_ref,
    inv_t,
    noise_raw,
    noise_ref,
    droot_ref,
    change_ref,
    ebuf,
    part,
    r1,
    rx,
    acc,
    full,
    meanp,
    stash,
    in_sem,
    out_sem,
    after_sem,
    p1s,
    p1r,
    xs,
    xr,
    fs,
    fr,
    zs,
    zr,
):
    n_ind, n_mark, n_chip, chunks, stops, count, block, levels = cfg
    tc = ebuf.shape[2]
    half = block // 2
    nb = half // LANES // levels
    seg_rows = nb * tc
    body_rows = levels * seg_rows
    groups = tc // SUB
    ind = lax.axis_index("ind")
    mark = lax.axis_index("mark")
    y = lax.axis_index("chip")
    core = lax.rem(ind, 2)
    x = lax.div(ind, 2)
    role = lax.rem(core + x + y, 2)
    other = 1 - role
    partner = {"ind": ind + 1 - 2 * core}
    nxt = {"mark": lax.rem(mark + 1, n_mark)}
    prv = {"mark": lax.rem(mark + n_mark - 1, n_mark)}

    def peer(axis, s):
        nx, ny = x, y
        if axis == "x":
            nx = x + s * (1 - 2 * lax.rem(lax.div(x, s), 2))
        else:
            ny = y + s * (1 - 2 * lax.rem(lax.div(y, s), 2))
        return {"ind": nx * 2 + lax.rem(role + nx + ny, 2), "chip": ny}

    peers = [peer("x", s) for s in bits_of(n_ind // 2)] + [peer("y", s) for s in bits_of(n_chip)]

    blocks = geno_ref.shape[0]
    per_visit = chunks // blocks
    piece = noise_ref.shape[3]
    loads = [pltpu.make_async_copy(resid_hbm, resid_ref, in_sem.at[0])]
    for k in range(blocks):
        loads.append(
            pltpu.make_async_copy(
                geno_hbm.at[:, k * block : (k + 1) * block], geno_ref.at[k], in_sem.at[1 + k]
            )
        )
    loads.append(pltpu.make_async_copy(noise_hbm, noise_raw, in_sem.at[1 + blocks]))
    loads.append(pltpu.make_async_copy(inv_hbm, inv_ref, in_sem.at[2 + blocks]))
    for load in loads:
        load.start()

    barrier = pltpu.get_barrier_semaphore()
    for dev in [partner, nxt, prv] + peers:
        pl.semaphore_signal(barrier, inc=1, device_id=dev, device_id_type=MESH)

    loads[0].wait()
    flipped = resid_ref[...].T
    for c in range(chunks):
        ebuf[0, c] = flipped[c * tc : (c + 1) * tc]
    for k in range(blocks):
        loads[1 + k].wait()
    pl.semaphore_wait(barrier, 3 + levels)

    def copy(src, dst, ssem, rsem, dev):
        return pltpu.make_async_remote_copy(
            src_ref=src, dst_ref=dst, send_sem=ssem, recv_sem=rsem, device_id=dev, device_id_type=MESH
        )

    def hop(stop, c):
        return copy(ebuf.at[stop, c], ebuf.at[stop + 1, c], zs.at[stop, c], zr.at[stop, c], nxt)

    def pair(c):
        return copy(part.at[c, other], r1.at[c], p1s.at[c], p1r.at[c], partner)

    def rows_of(g):
        return pl.ds(g * seg_rows, seg_rows + (SUB if g == levels - 1 else 0))

    def source(c, p):
        return part.at[c, role] if p == 0 else acc.at[c, p - 1]

    def swap(c, p, g):
        rows = rows_of(g)
        return copy(
            source(c, p).at[rows], rx.at[c, p, rows], xs.at[c, p, g], xr.at[c, p, g], peers[(g + p) % levels]
        )

    def forward(c):
        return copy(
            full.at[c, role, pl.ds(0, body_rows)],
            full.at[c, role, pl.ds(0, body_rows)],
            fs.at[c],
            fr.at[c],
            partner,
        )

    lane = lax.broadcasted_iota(jnp.int32, (SUB, LANES), 1)

    def bit(s):
        return lax.rem(lax.div(lane, s), 2) == 1

    def fold(tot):
        parts = [tot[SUB * g : SUB * (g + 1)] for g in range(groups)]
        s = LANES // 2
        while len(parts) > 1:
            take = bit(s)
            parts = [
                jnp.where(take, a + pltpu.roll(a, s, 1), b + pltpu.roll(b, LANES - s, 1))
                for a, b in zip(parts[::2], parts[1::2])
            ]
            s //= 2
        return parts[0]

    def unfold(tile):
        sums = []
        for g in range(groups):
            s, r, value = LANES // 2, g, tile
            for _ in bits_of(groups):
                value = jnp.where(bit(s) if r % 2 == 0 else jnp.logical_not(bit(s)), value, 0.0)
                s, r = s // 2, r // 2
            sums.append(jnp.sum(value, axis=1, keepdims=True))
        return jnp.concatenate(sums, axis=0)

    def put(c, h, s):
        for i in range(levels * nb):
            part[c, h, i * tc : (i + 1) * tc, :] = s[:, i * LANES : (i + 1) * LANES]

    def scaled_half(c, h):
        return jnp.concatenate(
            [(full[c, h, i * tc : (i + 1) * tc, :] * (1.0 / count)).astype(jnp.bfloat16) for i in range(levels * nb)],
            axis=1,
        )

    def span(h):
        return pl.ds(pl.multiple_of(h * half, half), half)

    def score(stop, j, c):
        k = order_ref[stop, 0, j]
        e = ebuf[stop, c]
        eb = e.astype(jnp.bfloat16)
        put(c, other, jnp.dot(eb, geno_ref[k, :, span(other)], preferred_element_type=jnp.float32))
        sq = e * e
        tot = sq[:, :LANES]
        for i in range(1, sq.shape[1] // LANES):
            tot = tot + sq[:, i * LANES : (i + 1) * LANES]
        tile = fold(tot)
        part[c, 0, body_rows:, :] = tile
        part[c, 1, body_rows:, :] = tile
        pair(c).start()
        put(c, role, jnp.dot(eb, geno_ref[k, :, span(role)], preferred_element_type=jnp.float32))

    def phase_a(stop, c):
        @pl.when(stop > 0)
        def _():
            hop(stop - 1, c).wait_recv()

        score(stop, 0, c)

    def phase_b(stop, c):
        pair(c).wait_recv()
        part[c, role] = part[c, role] + r1[c]
        for g in range(levels):
            swap(c, 0, g).start()

    def phase_c(stop, c):
        for p in range(levels - 1):
            for g in range(levels):
                swap(c, p, g).wait_recv()
            acc[c, p] = source(c, p)[...] + rx[c, p]
            for g in range(levels):
                swap(c, p + 1, g).start()
        pair(c).wait_send()

    def phase_d(stop, j, c):
        p = levels - 1
        for g in range(levels):
            swap(c, p, g).wait_recv()
        full[c, role] = source(c, p)[...] + rx[c, p]
        forward(c).start()
        k = order_ref[stop, 0, j]
        meanp[c] = jnp.dot(scaled_half(c, role), inv_t[k, span(role), :], preferred_element_type=jnp.float32)
        for p in range(levels):
            for g in range(levels):
                swap(c, p, g).wait_send()

    def phase_e(stop, j, c):
        k = order_ref[stop, 0, j]
        spread = unfold(full[c, role, body_rows:, :]) * (1.0 / count)
        root = jnp.sqrt((spread + epsilon) * (1.0 / count))
        noise = jnp.concatenate(
            [
                noise_ref[stop, j * per_visit + i, pl.ds(pl.multiple_of(c * tc, tc), tc), :]
                for i in range(per_visit)
            ],
            axis=1,
        ).astype(jnp.float32)
        forward(c).wait_recv()
        mean = meanp[c] + jnp.dot(
            scaled_half(c, other), inv_t[k, span(other), :], preferred_element_type=jnp.float32
        )
        change = mean + (root * droot_ref[k]) * noise
        stash[c, j] = change
        ebuf[stop, c] = ebuf[stop, c] - jnp.dot(
            change.astype(jnp.bfloat16), geno_t[k], preferred_element_type=jnp.float32
        )

    def at(x, fn):
        stop, c = lax.div(x, PERIOD), lax.rem(x, PERIOD)

        @pl.when((x >= 0) & (c < chunks) & (stop < stops))
        def _():
            fn(stop, c)

    def out_copy(stop, c):
        return pltpu.make_async_copy(change_ref.at[stop, :, c], change_hbm.at[stop, :, c], out_sem.at[stop, c])

    def last(stop, c):
        phase_e(stop, 1, c)
        hop(stop, c).start()
        forward(c).wait_send()
        first = order_ref[stop, 0, 0]
        change_ref[stop, 0, c] = stash[c, first]
        change_ref[stop, 1, c] = stash[c, 1 - first]
        out_copy(stop, c).start()

    def middle(stop, c):
        phase_e(stop, 0, c)
        score(stop, 1, c)
        forward(c).wait_send()

    def flip(stop, i):
        noise_ref[stop, i] = noise_raw[stop, pl.ds(pl.multiple_of(i * piece, piece), piece), :].T

    def turn(src, dst):
        for k in range(blocks):

            def one(i, z):
                cols = pl.ds(pl.multiple_of(i * LANES, LANES), LANES)
                dst[k, cols, :] = src[k, :, cols].T
                return z

            lax.fori_loop(0, block // LANES, one, 0)

    def prepare_noise():
        loads[1 + blocks].wait()
        lax.fori_loop(0, chunks, lambda i, x: (flip(0, i), x)[1], 0)

    def prepare_inverse():
        loads[2 + blocks].wait()
        turn(inv_ref, inv_t)
        eye = lax.broadcasted_iota(jnp.int32, (LANES, LANES), 0) == lax.broadcasted_iota(
            jnp.int32, (LANES, LANES), 1
        )
        for k in range(blocks):
            for i in range(0, block, LANES):
                tile = inv_ref[k, i : i + LANES, i : i + LANES].astype(jnp.float32)
                diag = jnp.sum(jnp.where(eye, tile, 0.0), axis=0, keepdims=True)
                droot_ref[k, :, i : i + LANES] = jnp.sqrt(diag)

    def prepare_genotypes():
        turn(geno_ref, geno_t)

    once = {"N": prepare_noise, "V": prepare_inverse, "G": prepare_genotypes}
    phases = {
        "a": phase_a,
        "b": phase_b,
        "c": phase_c,
        "d": lambda stop, c: phase_d(stop, 0, c),
        "e": lambda stop, c: phase_d(stop, 1, c),
        "m": middle,
        "l": last,
    }

    def body(t, carry):
        for name, delay in ORDER:
            if name in once:
                pl.when(t == delay)(once[name])
            else:
                at(t - delay, phases[name])
        at(t + PERIOD, flip)
        return carry

    lax.fori_loop(0, PERIOD * (stops - 1) + chunks + max(delay for _, delay in ORDER), body, 0)

    def finish(c):
        return pltpu.make_async_copy(ebuf.at[stops, c], after_hbm.at[c], after_sem.at[c])

    for c in range(chunks):
        hop(stops - 1, c).wait_recv()
        finish(c).start()
    for c in range(chunks):
        for stop in range(stops):
            out_copy(stop, c).wait()
            hop(stop, c).wait_send()
        finish(c).wait()


def local(mesh_shape, genotypes, residual, posterior_inverse, gibbs_noise, visit_order):
    n_ind, n_mark, n_chip = mesh_shape
    levels = len(bits_of(n_ind // 2)) + len(bits_of(n_chip))
    people, traits = residual.shape
    count = people * n_ind * n_chip
    blocks, block = posterior_inverse.shape[:2]
    stops = gibbs_noise.shape[0]
    chunks = CHUNKS
    tc = traits // chunks
    rows = block // 2 // LANES * tc + SUB
    f32, bf16 = jnp.float32, jnp.bfloat16
    cfg = (n_ind, n_mark, n_chip, chunks, stops, count, block, levels)
    hbm = pl.BlockSpec(memory_space=pl.ANY)
    dma = pltpu.SemaphoreType.DMA
    after, changes = pl.pallas_call(
        functools.partial(kernel, cfg),
        out_shape=(
            jax.ShapeDtypeStruct((chunks, tc, people), f32),
            jax.ShapeDtypeStruct((stops, blocks, chunks, tc, block), f32),
        ),
        in_specs=[pl.BlockSpec(memory_space=pltpu.SMEM)] + [hbm] * 4,
        out_specs=(hbm, hbm),
        scratch_shapes=[
            pltpu.VMEM((blocks, people, block), bf16),
            pltpu.VMEM((blocks, block, people), bf16),
            pltpu.VMEM((people, traits), f32),
            pltpu.VMEM((blocks, block, block), bf16),
            pltpu.VMEM((blocks, block, block), bf16),
            pltpu.VMEM((stops, blocks * block, traits), bf16),
            pltpu.VMEM((stops, chunks, traits, blocks * block // chunks), bf16),
            pltpu.VMEM((blocks, 1, block), f32),
            pltpu.VMEM((stops, blocks, chunks, tc, block), f32),
            pltpu.VMEM((stops + 1, chunks, tc, people), f32),
            pltpu.VMEM((chunks, 2, rows, LANES), f32),
            pltpu.VMEM((chunks, rows, LANES), f32),
            pltpu.VMEM((chunks, levels, rows, LANES), f32),
            pltpu.VMEM((chunks, levels - 1, rows, LANES), f32),
            pltpu.VMEM((chunks, 2, rows, LANES), f32),
            pltpu.VMEM((chunks, tc, block), f32),
            pltpu.VMEM((chunks, blocks, tc, block), f32),
            dma((3 + blocks,)),
            dma((stops, chunks)),
            dma((chunks,)),
            dma((chunks,)),
            dma((chunks,)),
            dma((chunks, levels, levels)),
            dma((chunks, levels, levels)),
            dma((chunks,)),
            dma((chunks,)),
            dma((stops, chunks)),
            dma((stops, chunks)),
        ],
        compiler_params=pltpu.CompilerParams(
            collective_id=0, has_side_effects=True, vmem_limit_bytes=60 * 1024 * 1024
        ),
    )(visit_order, genotypes, residual, posterior_inverse, gibbs_noise)
    after = after.reshape(traits, people).T
    changes = changes.reshape(stops, blocks, traits, block).transpose(0, 1, 3, 2)
    return after, changes.reshape(stops, blocks * block, traits)


def solution(mesh):
    in_specs = (
        P(("ind", "chip"), "mark"),
        P(("ind", "chip"), "mark"),
        P("mark", None, None),
        P(None, "mark", None),
        P(None, "mark", None),
    )
    out_specs = (P(("ind", "chip"), "mark"), P(None, "mark", None))
    shape = (mesh.shape["ind"], mesh.shape["mark"], mesh.shape["chip"])
    return jax.shard_map(
        functools.partial(local, shape), mesh=mesh, in_specs=in_specs, out_specs=out_specs, check_vma=False
    )
```

```python
import functools

import jax
import jax.numpy as jnp
from jax import lax
from jax.experimental import pallas as pl
from jax.experimental.pallas import tpu as pltpu
from jax.sharding import PartitionSpec as P

epsilon = 1e-05
MESH = pl.DeviceIdType.MESH
CHUNKS = 8
PERIOD = 10
ORDER = (
    ("c", 2),
    ("a", 0),
    ("N", 0),
    ("V", 2),
    ("d", 3),
    ("b", 4),
    ("l", 7),
    ("c", 5),
    ("G", 1),
    ("b", 0),
    ("m", 3),
    ("e", 6),
)
LANES = 128
SUB = 8


def bits_of(n):
    steps = []
    s = 1
    while s < n:
        steps.append(s)
        s *= 2
    return steps


def kernel(
    cfg,
    order_ref,
    geno_hbm,
    resid_hbm,
    inv_hbm,
    noise_hbm,
    after_hbm,
    change_hbm,
    geno_ref,
    geno_t,
    resid_ref,
    inv_ref,
    inv_t,
    noise_raw,
    noise_ref,
    droot_ref,
    change_ref,
    ebuf,
    part,
    r1,
    rx,
    acc,
    full,
    meanp,
    stash,
    in_sem,
    out_sem,
    after_sem,
    p1s,
    p1r,
    xs,
    xr,
    fs,
    fr,
    zs,
    zr,
):
    n_ind, n_mark, n_chip, chunks, stops, count, block, levels = cfg
    tc = ebuf.shape[2]
    half = block // 2
    nb = half // LANES // levels
    seg_rows = nb * tc
    body_rows = levels * seg_rows
    groups = tc // SUB
    ind = lax.axis_index("ind")
    mark = lax.axis_index("mark")
    y = lax.axis_index("chip")
    core = lax.rem(ind, 2)
    x = lax.div(ind, 2)
    role = lax.rem(core + x + y, 2)
    other = 1 - role
    partner = {"ind": ind + 1 - 2 * core}
    nxt = {"mark": lax.rem(mark + 1, n_mark)}
    prv = {"mark": lax.rem(mark + n_mark - 1, n_mark)}

    def peer(axis, s):
        nx, ny = x, y
        if axis == "x":
            nx = x + s * (1 - 2 * lax.rem(lax.div(x, s), 2))
        else:
            ny = y + s * (1 - 2 * lax.rem(lax.div(y, s), 2))
        return {"ind": nx * 2 + lax.rem(role + nx + ny, 2), "chip": ny}

    peers = [peer("x", s) for s in bits_of(n_ind // 2)] + [peer("y", s) for s in bits_of(n_chip)]

    blocks = geno_ref.shape[0]
    per_visit = chunks // blocks
    piece = noise_ref.shape[3]
    loads = [pltpu.make_async_copy(resid_hbm, resid_ref, in_sem.at[0])]
    for k in range(blocks):
        loads.append(
            pltpu.make_async_copy(
                geno_hbm.at[:, k * block : (k + 1) * block], geno_ref.at[k], in_sem.at[1 + k]
            )
        )
    loads.append(pltpu.make_async_copy(noise_hbm, noise_raw, in_sem.at[1 + blocks]))
    loads.append(pltpu.make_async_copy(inv_hbm, inv_ref, in_sem.at[2 + blocks]))
    for load in loads:
        load.start()

    barrier = pltpu.get_barrier_semaphore()
    for dev in [partner, nxt, prv] + peers:
        pl.semaphore_signal(barrier, inc=1, device_id=dev, device_id_type=MESH)

    loads[0].wait()
    flipped = resid_ref[...].T
    for c in range(chunks):
        ebuf[0, c] = flipped[c * tc : (c + 1) * tc]
    for k in range(blocks):
        loads[1 + k].wait()
    pl.semaphore_wait(barrier, 3 + levels)

    def copy(src, dst, ssem, rsem, dev):
        return pltpu.make_async_remote_copy(
            src_ref=src, dst_ref=dst, send_sem=ssem, recv_sem=rsem, device_id=dev, device_id_type=MESH
        )

    def hop(stop, c):
        return copy(ebuf.at[stop, c], ebuf.at[stop + 1, c], zs.at[stop, c], zr.at[stop, c], nxt)

    def pair(c):
        return copy(part.at[c, other], r1.at[c], p1s.at[c], p1r.at[c], partner)

    def rows_of(g):
        return pl.ds(g * seg_rows, seg_rows + (SUB if g == levels - 1 else 0))

    def source(c, p):
        return part.at[c, role] if p == 0 else acc.at[c, p - 1]

    def swap(c, p, g):
        rows = rows_of(g)
        return copy(
            source(c, p).at[rows], rx.at[c, p, rows], xs.at[c, p, g], xr.at[c, p, g], peers[(g + p) % levels]
        )

    def forward(c):
        return copy(
            full.at[c, role, pl.ds(0, body_rows)],
            full.at[c, role, pl.ds(0, body_rows)],
            fs.at[c],
            fr.at[c],
            partner,
        )

    lane = lax.broadcasted_iota(jnp.int32, (SUB, LANES), 1)

    def bit(s):
        return lax.rem(lax.div(lane, s), 2) == 1

    def fold(tot):
        parts = [tot[SUB * g : SUB * (g + 1)] for g in range(groups)]
        s = LANES // 2
        while len(parts) > 1:
            take = bit(s)
            parts = [
                jnp.where(take, a + pltpu.roll(a, s, 1), b + pltpu.roll(b, LANES - s, 1))
                for a, b in zip(parts[::2], parts[1::2])
            ]
            s //= 2
        return parts[0]

    def unfold(tile):
        sums = []
        for g in range(groups):
            s, r, value = LANES // 2, g, tile
            for _ in bits_of(groups):
                value = jnp.where(bit(s) if r % 2 == 0 else jnp.logical_not(bit(s)), value, 0.0)
                s, r = s // 2, r // 2
            sums.append(jnp.sum(value, axis=1, keepdims=True))
        return jnp.concatenate(sums, axis=0)

    def put(c, h, s):
        for i in range(levels * nb):
            part[c, h, i * tc : (i + 1) * tc, :] = s[:, i * LANES : (i + 1) * LANES]

    def scaled_half(c, h):
        return jnp.concatenate(
            [(full[c, h, i * tc : (i + 1) * tc, :] * (1.0 / count)).astype(jnp.bfloat16) for i in range(levels * nb)],
            axis=1,
        )

    def span(h):
        return pl.ds(pl.multiple_of(h * half, half), half)

    def score(stop, j, c):
        k = order_ref[stop, 0, j]
        e = ebuf[stop, c]
        eb = e.astype(jnp.bfloat16)
        put(c, other, jnp.dot(eb, geno_ref[k, :, span(other)], preferred_element_type=jnp.float32))
        sq = e * e
        tot = sq[:, :LANES]
        for i in range(1, sq.shape[1] // LANES):
            tot = tot + sq[:, i * LANES : (i + 1) * LANES]
        tile = fold(tot)
        part[c, 0, body_rows:, :] = tile
        part[c, 1, body_rows:, :] = tile
        pair(c).start()
        put(c, role, jnp.dot(eb, geno_ref[k, :, span(role)], preferred_element_type=jnp.float32))

    def phase_a(stop, c):
        @pl.when(stop > 0)
        def _():
            hop(stop - 1, c).wait_recv()

        score(stop, 0, c)

    def phase_b(stop, c):
        pair(c).wait_recv()
        part[c, role] = part[c, role] + r1[c]
        for g in range(levels):
            swap(c, 0, g).start()

    def phase_c(stop, c):
        for p in range(levels - 1):
            for g in range(levels):
                swap(c, p, g).wait_recv()
            acc[c, p] = source(c, p)[...] + rx[c, p]
            for g in range(levels):
                swap(c, p + 1, g).start()
        pair(c).wait_send()

    def phase_d(stop, j, c):
        p = levels - 1
        for g in range(levels):
            swap(c, p, g).wait_recv()
        full[c, role] = source(c, p)[...] + rx[c, p]
        forward(c).start()
        k = order_ref[stop, 0, j]
        meanp[c] = jnp.dot(scaled_half(c, role), inv_t[k, span(role), :], preferred_element_type=jnp.float32)
        for p in range(levels):
            for g in range(levels):
                swap(c, p, g).wait_send()

    def phase_e(stop, j, c):
        k = order_ref[stop, 0, j]
        spread = unfold(full[c, role, body_rows:, :]) * (1.0 / count)
        root = jnp.sqrt((spread + epsilon) * (1.0 / count))
        noise = jnp.concatenate(
            [
                noise_ref[stop, j * per_visit + i, pl.ds(pl.multiple_of(c * tc, tc), tc), :]
                for i in range(per_visit)
            ],
            axis=1,
        ).astype(jnp.float32)
        forward(c).wait_recv()
        mean = meanp[c] + jnp.dot(
            scaled_half(c, other), inv_t[k, span(other), :], preferred_element_type=jnp.float32
        )
        change = mean + (root * droot_ref[k]) * noise
        stash[c, j] = change
        ebuf[stop, c] = ebuf[stop, c] - jnp.dot(
            change.astype(jnp.bfloat16), geno_t[k], preferred_element_type=jnp.float32
        )

    def at(x, fn):
        stop, c = lax.div(x, PERIOD), lax.rem(x, PERIOD)

        @pl.when((x >= 0) & (c < chunks) & (stop < stops))
        def _():
            fn(stop, c)

    def out_copy(stop, c):
        return pltpu.make_async_copy(change_ref.at[stop, :, c], change_hbm.at[stop, :, c], out_sem.at[stop, c])

    def last(stop, c):
        phase_e(stop, 1, c)
        hop(stop, c).start()
        forward(c).wait_send()
        first = order_ref[stop, 0, 0]
        change_ref[stop, 0, c] = stash[c, first]
        change_ref[stop, 1, c] = stash[c, 1 - first]
        out_copy(stop, c).start()

    def middle(stop, c):
        phase_e(stop, 0, c)
        score(stop, 1, c)
        forward(c).wait_send()

    def flip(stop, i):
        noise_ref[stop, i] = noise_raw[stop, pl.ds(pl.multiple_of(i * piece, piece), piece), :].T

    def turn(src, dst):
        for k in range(blocks):

            def one(i, z):
                cols = pl.ds(pl.multiple_of(i * LANES, LANES), LANES)
                dst[k, cols, :] = src[k, :, cols].T
                return z

            lax.fori_loop(0, block // LANES, one, 0)

    def prepare_noise():
        loads[1 + blocks].wait()
        lax.fori_loop(0, chunks, lambda i, x: (flip(0, i), x)[1], 0)

    def prepare_inverse():
        loads[2 + blocks].wait()
        turn(inv_ref, inv_t)
        eye = lax.broadcasted_iota(jnp.int32, (LANES, LANES), 0) == lax.broadcasted_iota(
            jnp.int32, (LANES, LANES), 1
        )
        for k in range(blocks):
            for i in range(0, block, LANES):
                tile = inv_ref[k, i : i + LANES, i : i + LANES].astype(jnp.float32)
                diag = jnp.sum(jnp.where(eye, tile, 0.0), axis=0, keepdims=True)
                droot_ref[k, :, i : i + LANES] = jnp.sqrt(diag)

    def prepare_genotypes():
        turn(geno_ref, geno_t)

    once = {"N": prepare_noise, "V": prepare_inverse, "G": prepare_genotypes}
    phases = {
        "a": phase_a,
        "b": phase_b,
        "c": phase_c,
        "d": lambda stop, c: phase_d(stop, 0, c),
        "e": lambda stop, c: phase_d(stop, 1, c),
        "m": middle,
        "l": last,
    }

    def body(t, carry):
        for name, delay in ORDER:
            if name in once:
                pl.when(t == delay)(once[name])
            else:
                at(t - delay, phases[name])
        at(t + PERIOD, flip)
        return carry

    lax.fori_loop(0, PERIOD * (stops - 1) + chunks + max(delay for _, delay in ORDER), body, 0)

    def finish(c):
        return pltpu.make_async_copy(ebuf.at[stops, c], after_hbm.at[c], after_sem.at[c])

    for c in range(chunks):
        hop(stops - 1, c).wait_recv()
        finish(c).start()
    for c in range(chunks):
        for stop in range(stops):
            out_copy(stop, c).wait()
            hop(stop, c).wait_send()
        finish(c).wait()


def local(mesh_shape, genotypes, residual, posterior_inverse, gibbs_noise, visit_order):
    n_ind, n_mark, n_chip = mesh_shape
    levels = len(bits_of(n_ind // 2)) + len(bits_of(n_chip))
    people, traits = residual.shape
    count = people * n_ind * n_chip
    blocks, block = posterior_inverse.shape[:2]
    stops = gibbs_noise.shape[0]
    chunks = CHUNKS
    tc = traits // chunks
    rows = block // 2 // LANES * tc + SUB
    f32, bf16 = jnp.float32, jnp.bfloat16
    cfg = (n_ind, n_mark, n_chip, chunks, stops, count, block, levels)
    hbm = pl.BlockSpec(memory_space=pl.ANY)
    dma = pltpu.SemaphoreType.DMA
    after, changes = pl.pallas_call(
        functools.partial(kernel, cfg),
        out_shape=(
            jax.ShapeDtypeStruct((chunks, tc, people), f32),
            jax.ShapeDtypeStruct((stops, blocks, chunks, tc, block), f32),
        ),
        in_specs=[pl.BlockSpec(memory_space=pltpu.SMEM)] + [hbm] * 4,
        out_specs=(hbm, hbm),
        scratch_shapes=[
            pltpu.VMEM((blocks, people, block), bf16),
            pltpu.VMEM((blocks, block, people), bf16),
            pltpu.VMEM((people, traits), f32),
            pltpu.VMEM((blocks, block, block), bf16),
            pltpu.VMEM((blocks, block, block), bf16),
            pltpu.VMEM((stops, blocks * block, traits), bf16),
            pltpu.VMEM((stops, chunks, traits, blocks * block // chunks), bf16),
            pltpu.VMEM((blocks, 1, block), f32),
            pltpu.VMEM((stops, blocks, chunks, tc, block), f32),
            pltpu.VMEM((stops + 1, chunks, tc, people), f32),
            pltpu.VMEM((chunks, 2, rows, LANES), f32),
            pltpu.VMEM((chunks, rows, LANES), f32),
            pltpu.VMEM((chunks, levels, rows, LANES), f32),
            pltpu.VMEM((chunks, levels - 1, rows, LANES), f32),
            pltpu.VMEM((chunks, 2, rows, LANES), f32),
            pltpu.VMEM((chunks, tc, block), f32),
            pltpu.VMEM((chunks, blocks, tc, block), f32),
            dma((3 + blocks,)),
            dma((stops, chunks)),
            dma((chunks,)),
            dma((chunks,)),
            dma((chunks,)),
            dma((chunks, levels, levels)),
            dma((chunks, levels, levels)),
            dma((chunks,)),
            dma((chunks,)),
            dma((stops, chunks)),
            dma((stops, chunks)),
        ],
        compiler_params=pltpu.CompilerParams(
            collective_id=0, has_side_effects=True, vmem_limit_bytes=60 * 1024 * 1024
        ),
    )(visit_order, genotypes, residual, posterior_inverse, gibbs_noise)
    after = after.reshape(traits, people).T
    changes = changes.reshape(stops, blocks, traits, block).transpose(0, 1, 3, 2)
    return after, changes.reshape(stops, blocks * block, traits)


def solution(mesh):
    in_specs = (
        P(("ind", "chip"), "mark"),
        P(("ind", "chip"), "mark"),
        P("mark", None, None),
        P(None, "mark", None),
        P(None, "mark", None),
    )
    out_specs = (P(("ind", "chip"), "mark"), P(None, "mark", None))
    shape = (mesh.shape["ind"], mesh.shape["mark"], mesh.shape["chip"])
    return jax.shard_map(
        functools.partial(local, shape), mesh=mesh, in_specs=in_specs, out_specs=out_specs, check_vma=False
    )
```
